512 devices in a mesh: src: 32 (over x, y), col: 16 (over z, core).
Axes of the slice: x: 4, y: 8, z: 8, core: 2. Of those that a mesh axis runs over, the one named last changes fastest.
Arguments:
- perambulator: bfloat16 [32, 16, 2, 768, 768], P('src', None, None, 'col'), may hold values from -0.15625 to 0.15625
- elementals: bfloat16 [16, 4, 2, 192, 192], P('col'), may hold values from -0.3125 to 0.3125
- sink_block: bfloat16 [2, 768, 128], replicated, may hold values from -6 to 6
- gamma_spin: float32 [2, 4, 4], replicated, may hold values from -2.5 to 2.5
- graph_lists: int32 [32, 6, 3], P('src'), may hold values from 0 to 31, as said below
- diagram_counts: int32 [32], P('src'), may hold values from 1 to 6, as said below
- source_ids: int32 [32], P('src'), may hold values from 0 to 3
Outputs:
- contraction: float32 [32, 16, 6, 2, 128, 128], P('src', 'col')
The draws below stay inside these ranges and needn't reach their ends.
Inputs may be any that keep to these rules, and one draw needn't show every extreme that they name: `graph_lists`: both senders of a slot of receiver t lie within 2 of t; in slot 0 the first sender is t - 2 and the second t + 2 where these exist (else t + 2, t - 2); the third entry is below 4; every slot holds valid entries. `diagram_counts`: at least one source time has exactly 6 live slots.
All inputs are finite; a program needn't handle non-finite values.
Results may differ from the reference program's by a relative error of at most 0.018.
Values may be sent and summed in bfloat16 or wider, within the bound.
No kernel may reach another device: no remote copies, remote signals or barrier semaphores. Data moves between devices by JAX's collectives and lax.ppermute only.
A program may use at most 64 MiB of HBM per device.

```python
import jax
import jax.numpy as jnp
from jax import lax

NEV = 192
NDIM = 768
COLS = 128
NMOM = 4
DT = 2
DMAX = 6
TSRC = 32
SINKS = 16


def draw_graph_lists(key, part):
    base = jax.random.fold_in(key, 11)
    key_first, key_second, key_ident = jax.random.split(base, 3)
    receiver = jnp.arange(TSRC, dtype=jnp.int32)[:, None]
    first = jnp.clip(receiver + jax.random.randint(key_first, (TSRC, DMAX), -DT, DT + 1), 0, TSRC - 1)
    second = jnp.clip(receiver + jax.random.randint(key_second, (TSRC, DMAX), -DT, DT + 1), 0, TSRC - 1)
    lower = jnp.where(receiver[:, 0] >= DT, receiver[:, 0] - DT, receiver[:, 0] + DT)
    upper = jnp.where(receiver[:, 0] + DT <= TSRC - 1, receiver[:, 0] + DT, receiver[:, 0] - DT)
    first = first.at[:, 0].set(lower)
    second = second.at[:, 0].set(upper)
    ident = jax.random.randint(key_ident, (TSRC, DMAX), 0, NMOM)
    return jnp.stack([first, second, ident], axis=2).astype(jnp.int32)


def draw_diagram_counts(key, part):
    base = jax.random.fold_in(key, 23)
    key_low, key_busy, key_place = jax.random.split(base, 3)
    counts = jax.random.randint(key_low, (TSRC,), 1, 3)
    busy = jax.random.randint(key_busy, (TSRC,), 0, 8) == 0
    counts = jnp.where(busy, DMAX, counts)
    place = jax.random.randint(key_place, (), 0, TSRC)
    return counts.at[place].set(DMAX).astype(jnp.int32)


def touch_ends(array, rng, smallest, high):
    spot = [jax.random.randint(jax.random.fold_in(rng, axis), (), 0, length) for axis, length in enumerate(array.shape)]
    main_axis = array.shape.index(max(array.shape))
    beside = spot[:main_axis] + [(spot[main_axis] + 1) % array.shape[main_axis]] + spot[main_axis + 1:]
    return array.at[tuple(spot)].set(smallest).at[tuple(beside)].set(high)


def block_levels(rng, dims, shards, least, high):
    def one(position, parts):
        heights = jax.random.uniform(jax.random.fold_in(jax.random.fold_in(rng, 6), position), (parts,), jnp.float32, least / len(shards), high / len(shards))
        return jnp.repeat(jnp.exp(heights), dims[position] // parts).reshape((-1,) + (1,) * (len(dims) - position - 1))

    factor_of = one(*shards[0])
    for cut in shards[1:]:
        factor_of = factor_of * one(*cut)
    return factor_of


def bell_draw(key, shape, scale, limit, pieces=(), kind=jnp.bfloat16):
    gain = block_levels(key, shape, pieces, -0.22, 0.18) if pieces else 1.0
    drawn = jax.random.normal(key, shape, jnp.float32) * scale * gain
    return jnp.minimum(jnp.maximum(drawn, -limit), limit).astype(kind)


def setup_inputs(seed: int = 0) -> dict:
    arg_keys = jax.random.split(jax.random.key(seed), 8)
    return {
        "perambulator": bell_draw(arg_keys[0], (TSRC, SINKS, 2, NDIM, NDIM), (2 * NDIM) ** -0.5, 0.15625, ((0, 32), (3, 16))),
        "elementals": bell_draw(arg_keys[1], (SINKS, NMOM, 2, NEV, NEV), (2 * NEV) ** -0.5, 0.3125, ((0, 16),)),
        "sink_block": bell_draw(arg_keys[2], (2, NDIM, COLS), 1.0, 6.0),
        "gamma_spin": bell_draw(arg_keys[3], (2, 4, 4), 0.35, 2.5, (), jnp.float32),
        "graph_lists": draw_graph_lists(jax.random.fold_in(arg_keys[7], 71), 0),
        "diagram_counts": draw_diagram_counts(jax.random.fold_in(arg_keys[7], 71), 0),
        "source_ids": touch_ends(jax.random.randint(arg_keys[6], (TSRC,), 0, NMOM), jax.random.fold_in(arg_keys[6], 1), 0, NMOM - 1).astype(jnp.int32),
    }


def complex_dot(left, right):
    real_part = jnp.dot(left[0], right[0], preferred_element_type=jnp.float32) - jnp.dot(left[1], right[1], preferred_element_type=jnp.float32)
    imag_part = jnp.dot(left[0], right[1], preferred_element_type=jnp.float32) + jnp.dot(left[1], right[0], preferred_element_type=jnp.float32)
    return jnp.stack([real_part, imag_part])


def contract_rows(first, second):
    return lax.dot_general(first, second, (((0,), (0,)), ((), ())), preferred_element_type=jnp.float32)


def adjoint_dot(left, right):
    real_part = contract_rows(left[0], right[0]) + contract_rows(left[1], right[1])
    imag_part = contract_rows(left[0], right[1]) - contract_rows(left[1], right[0])
    return jnp.stack([real_part, imag_part])


def transposed_dot(stored, right):
    real_part = contract_rows(stored[0], right[0]) - contract_rows(stored[1], right[1])
    imag_part = contract_rows(stored[0], right[1]) + contract_rows(stored[1], right[0])
    return jnp.stack([real_part, imag_part])


def conjugate_dot(stored, right):
    real_part = jnp.dot(stored[0], right[0], preferred_element_type=jnp.float32) + jnp.dot(stored[1], right[1], preferred_element_type=jnp.float32)
    imag_part = jnp.dot(stored[0], right[1], preferred_element_type=jnp.float32) - jnp.dot(stored[1], right[0], preferred_element_type=jnp.float32)
    return jnp.stack([real_part, imag_part])


def spin_mix(values, matrix):
    real_part = jnp.einsum("st,etk->esk", matrix[0], values[0]) - jnp.einsum("st,etk->esk", matrix[1], values[1])
    imag_part = jnp.einsum("st,etk->esk", matrix[0], values[1]) + jnp.einsum("st,etk->esk", matrix[1], values[0])
    return jnp.stack([real_part, imag_part])


def dress_forward(elemental, gamma_spin, block):
    nev = elemental.shape[1]
    width = block.shape[2]
    colour = complex_dot(elemental, block.reshape(2, nev, 4 * width))
    return spin_mix(colour.reshape(2, nev, 4, width), gamma_spin).reshape(2, nev * 4, width)


def dress_backward(elemental, gamma_adjoint, block):
    nev = elemental.shape[1]
    width = block.shape[2]
    colour = adjoint_dot(elemental, block.reshape(2, nev, 4 * width))
    return spin_mix(colour.reshape(2, nev, 4, width), gamma_adjoint).reshape(2, nev * 4, width)


def reference(perambulator, elementals, sink_block, gamma_spin, graph_lists, diagram_counts, source_ids):
    gamma_adjoint = jnp.stack([gamma_spin[0].T, -gamma_spin[1].T])
    scale = (2.0 * sink_block.shape[1]) ** -0.5
    slots = graph_lists.shape[1]

    def per_sink(sink):
        tau_sink = lax.dynamic_index_in_dim(perambulator, sink, 1, keepdims=False)
        table = lax.dynamic_index_in_dim(elementals, sink, 0, keepdims=False)

        def dress_one(inputs):
            matrix, ident = inputs
            prop = transposed_dot(matrix, sink_block).astype(jnp.bfloat16)
            return dress_forward(table[ident], gamma_spin, prop).astype(jnp.bfloat16)

        dressed = lax.map(dress_one, (tau_sink, source_ids))

        def receive(inputs):
            matrix, lists, count = inputs

            def one_slot(slot):
                entry = lists[slot]
                undressed = dress_backward(table[entry[2]], gamma_adjoint, dressed[entry[0]]).astype(jnp.bfloat16)
                carried = conjugate_dot(matrix, undressed).astype(jnp.bfloat16)
                result = adjoint_dot(dressed[entry[1]], carried) * scale
                return result * (slot < count).astype(jnp.float32)

            return lax.map(one_slot, jnp.arange(slots, dtype=jnp.int32))

        return lax.map(receive, (tau_sink, graph_lists, diagram_counts))

    every = lax.map(per_sink, jnp.arange(perambulator.shape[1], dtype=jnp.int32))
    return jnp.swapaxes(every, 0, 1)
```

```python
import functools

import jax
import jax.numpy as jnp
from jax import lax
from jax.experimental import pallas as pl
from jax.experimental.pallas import tpu as pltpu
from jax.sharding import PartitionSpec as P

DT = 2
BF = jnp.bfloat16
F32 = jnp.float32


def shifted(shard, axis, by):
    count = lax.axis_size(axis)
    pairs = [(i, i + by) for i in range(count) if 0 <= i + by < count]
    return lax.ppermute(shard, axis, pairs)


def dot(left, right):
    return jnp.dot(left, right, preferred_element_type=F32)


def mix(values_r, values_i, g_r, g_i):
    out_r = g_r[0] * values_r[0] - g_i[0] * values_i[0]
    out_i = g_r[0] * values_i[0] + g_i[0] * values_r[0]
    for s in range(1, 4):
        out_r += g_r[s] * values_r[s] - g_i[s] * values_i[s]
        out_i += g_r[s] * values_i[s] + g_i[s] * values_r[s]
    return out_r, out_i


def tau_times(rows, tau_r, tau_i):
    half = rows.shape[0] // 2
    by_r = dot(rows, tau_r)
    by_i = dot(rows, tau_i)
    return by_r[:half] - by_i[half:], by_r[half:] + by_i[:half]


def dress_kernel(ident, gamma, pieces, sink_rows, forward, out, split, mixed):
    chunks, _, depth, ndim = pieces.shape
    width = out.shape[2]
    nev = ndim // 4
    tau_r = pieces[:, 0].reshape(chunks * depth, ndim)
    tau_i = pieces[:, 1].reshape(chunks * depth, ndim)
    prop_r, prop_i = tau_times(sink_rows[...], tau_r, tau_i)
    split[0] = prop_r.astype(BF).astype(F32).T
    split[1] = prop_i.astype(BF).astype(F32).T
    part_r = [split[0, pl.ds(s, nev, stride=4), :] for s in range(4)]
    part_i = [split[1, pl.ds(s, nev, stride=4), :] for s in range(4)]
    for s in range(4):
        g_r = [gamma[0, s, q] for q in range(4)]
        g_i = [gamma[1, s, q] for q in range(4)]
        m_r, m_i = mix(part_r, part_i, g_r, g_i)
        at_r = slice(s * width, (s + 1) * width)
        at_i = slice((4 + s) * width, (5 + s) * width)
        mixed[:nev, at_r] = m_r.astype(BF)
        mixed[:nev, at_i] = m_i.astype(BF)
        mixed[nev:, at_r] = (-m_i).astype(BF)
        mixed[nev:, at_i] = m_r.astype(BF)
    done = dot(forward[ident[0]], mixed[...])
    for c in range(2):
        for s in range(4):
            split[c, pl.ds(s, nev, stride=4), :] = done[:, (4 * c + s) * width : (4 * c + s + 1) * width]
    out[...] = split[...].astype(BF)


def diagrams_kernel(
    lists, count, position, gamma, pieces, d0, d1, d2, d3, d4, backward, out, wide, mixed, split, column
):
    chunks, _, depth, ndim = pieces.shape
    blocks = (d0, d1, d2, d3, d4)
    width = d0.shape[2]
    nev = ndim // 4
    tau_r = pieces[:, 0].reshape(chunks * depth, ndim)
    tau_i = pieces[:, 1].reshape(chunks * depth, ndim)
    for d, block in enumerate(blocks):
        rows = jnp.concatenate([block[0].T, block[1].T], axis=0)
        w_r, w_i = tau_times(rows, tau_r, tau_i)
        wide[d, :, :ndim] = w_r.astype(BF)
        wide[d, :, ndim:] = w_i.astype(BF)
        split[...] = block[...].astype(F32)
        part_r = [split[0, pl.ds(s, nev, stride=4), :] for s in range(4)]
        part_i = [split[1, pl.ds(s, nev, stride=4), :] for s in range(4)]
        for s in range(4):
            g_r = [gamma[0, q, s] for q in range(4)]
            g_i = [-gamma[1, q, s] for q in range(4)]
            m_r, m_i = mix(part_r, part_i, g_r, g_i)
            at_r = slice(s * width, (s + 1) * width)
            at_i = slice((4 + s) * width, (5 + s) * width)
            mixed[d, :nev, at_r] = m_r.astype(BF)
            mixed[d, :nev, at_i] = m_i.astype(BF)
            mixed[d, nev:, at_r] = m_i.astype(BF)
            mixed[d, nev:, at_i] = (-m_r).astype(BF)
    scale = (2.0 * ndim) ** (-0.5)
    offset = DT - position[0]
    for k in range(out.shape[0]):
        first = lists[k, 0] + offset
        second = lists[k, 1] + offset
        done = dot(backward[lists[k, 2]], mixed[first])
        for c in range(2):
            for s in range(4):
                at = slice((4 * c + s) * width, (4 * c + s + 1) * width)
                split[c, pl.ds(s, nev, stride=4), :] = done[:, at]
        u_r = split[0].astype(BF)
        u_i = split[1].astype(BF)
        column[:ndim, :width] = u_r
        column[:ndim, width:] = u_i
        column[ndim:, :width] = u_i
        column[ndim:, width:] = -u_r
        result = dot(wide[second], column[...]) * scale
        result = jnp.where(k < count[0], result, 0.0)
        out[k, 0] = result[:, :width]
        out[k, 1] = result[:, width:]


def per_device(
    perambulator, elementals, sink_block, gamma_spin, graph_lists, diagram_counts, source_ids
):
    ndim, width = sink_block.shape[1:]
    slots = graph_lists.shape[1]
    nev = elementals.shape[3]
    row_block = lax.all_to_all(perambulator, "col", split_axis=1, concat_axis=1, tiled=True)
    pieces = row_block[0]
    table = elementals[0]
    sink_rows = jnp.swapaxes(sink_block, 1, 2).reshape(2 * width, ndim)
    forward = jnp.concatenate([table[:, 0], table[:, 1]], axis=2)
    backward = jnp.concatenate(
        [jnp.swapaxes(table[:, 0], 1, 2), jnp.swapaxes(table[:, 1], 1, 2)], axis=2
    )
    smem = pl.BlockSpec(memory_space=pltpu.SMEM)
    vmem = pl.BlockSpec(memory_space=pltpu.VMEM)
    dressed = pl.pallas_call(
        dress_kernel,
        out_shape=jax.ShapeDtypeStruct((2, ndim, width), BF),
        in_specs=[smem, smem, vmem, vmem, vmem],
        out_specs=vmem,
        scratch_shapes=[
            pltpu.VMEM((2, ndim, width), F32),
            pltpu.VMEM((2 * nev, 8 * width), BF),
        ],
        name="dress",
    )(source_ids, gamma_spin, pieces, sink_rows, forward)
    blocks = [dressed if d == DT else shifted(dressed, "src", DT - d) for d in range(2 * DT + 1)]
    position = lax.axis_index("src").astype(jnp.int32).reshape(1)
    totals = pl.pallas_call(
        diagrams_kernel,
        out_shape=jax.ShapeDtypeStruct((slots, 2, width, width), F32),
        in_specs=[smem] * 4 + [vmem] * 7,
        out_specs=vmem,
        scratch_shapes=[
            pltpu.VMEM((2 * DT + 1, width, 2 * ndim), BF),
            pltpu.VMEM((2 * DT + 1, 2 * nev, 8 * width), BF),
            pltpu.VMEM((2, ndim, width), F32),
            pltpu.VMEM((2 * ndim, 2 * width), BF),
        ],
        name="diagrams",
    )(graph_lists[0], diagram_counts, position, gamma_spin, pieces, *blocks, backward)
    return totals[None, None]


def solution(mesh):
    in_specs = (
        P("src", None, None, "col", None),
        P("col", None, None, None, None),
        P(),
        P(),
        P("src", None, None),
        P("src"),
        P("src"),
    )
    out_specs = P("src", "col", None, None, None, None)
    return jax.shard_map(
        per_device, mesh=mesh, in_specs=in_specs, out_specs=out_specs, check_vma=False
    )
```

```python
import jax
import jax.numpy as jnp
from jax import lax
from jax.experimental import pallas as pl
from jax.experimental.pallas import tpu as pltpu
from jax.sharding import PartitionSpec as P

DT = 2
TILE = 16
BF = jnp.bfloat16
F32 = jnp.float32


def shifted(shard, axis, by):
    count = lax.axis_size(axis)
    pairs = [(i, i + by) for i in range(count) if 0 <= i + by < count]
    return lax.ppermute(shard, axis, pairs)


def dot(left, right):
    return jnp.dot(left, right, preferred_element_type=F32)


def tau_copies(pieces, tau, sem):
    chunks, parts, depth, _ = pieces.shape
    return [
        pltpu.make_async_copy(
            pieces.at[c, part], tau.at[pl.ds((part * chunks + c) * depth, depth)], sem.at[part * chunks + c]
        )
        for part in range(parts)
        for c in range(chunks)
    ]


def spin_mix(split, gamma, adjoint, write, starts):
    for start in starts:
        part = [[split[c, pl.ds(4 * start + s, TILE, stride=4), :] for s in range(4)] for c in range(2)]
        for s in range(4):
            real = imag = None
            for q in range(4):
                if adjoint:
                    g_r, g_i = gamma[0, q, s], -gamma[1, q, s]
                else:
                    g_r, g_i = gamma[0, s, q], gamma[1, s, q]
                term_r = g_r * part[0][q] - g_i * part[1][q]
                term_i = g_r * part[1][q] + g_i * part[0][q]
                real = term_r if real is None else real + term_r
                imag = term_i if imag is None else imag + term_i
            write(start, s, real, imag)


def eigen_product(matrix, mixed, split, width):
    nev = matrix.shape[0]
    for c in range(2):
        for half in range(2):
            at = (2 * c + half) * 2 * width
            done = dot(matrix[...], mixed[:, at : at + 2 * width])
            for q in range(2):
                split[c, pl.ds(2 * half + q, nev, stride=4), :] = done[:, q * width : (q + 1) * width]


def dress_kernel(ident, gamma, pieces, sink_rows, forward, out, tau, split, mixed, sem):
    ndim, width = out.shape[1:]
    nev = ndim // 4
    copies = tau_copies(pieces, tau, sem)
    for copy in copies:
        copy.start()
    for copy in copies:
        copy.wait()
    for c in range(2):
        prop = dot(sink_rows[c * width : (c + 1) * width, :], tau[...])
        split[c] = prop.astype(BF).astype(F32).T

    def write(start, s, real, imag):
        rows = slice(start, start + TILE)
        low = slice(nev + start, nev + start + TILE)
        at_r = slice(s * width, (s + 1) * width)
        at_i = slice((4 + s) * width, (5 + s) * width)
        mixed[rows, at_r] = real.astype(BF)
        mixed[rows, at_i] = imag.astype(BF)
        mixed[low, at_r] = (-imag).astype(BF)
        mixed[low, at_i] = real.astype(BF)

    spin_mix(split, gamma, False, write, range(0, nev, TILE))
    eigen_product(forward.at[ident[0]], mixed, split, width)
    out[...] = split[...].astype(BF)


def diagrams_kernel(
    lists, count, position, gamma, pieces, d0, d1, d2, d3, d4, backward, out,
    tau, wide, mixed, rows, split, column, local, sem, block_sem,
):
    ndim, width = d0.shape[1:]
    nev = ndim // 4
    copies = tau_copies(pieces, tau, sem)
    blocks = [
        pltpu.make_async_copy(block, local.at[d], block_sem.at[d]) for d, block in enumerate((d0, d1, d2, d3, d4))
    ]
    for copy in blocks + copies:
        copy.start()
    for copy in blocks + copies:
        copy.wait()
    for d in range(2 * DT + 1):
        left = local[d, 0].T
        right = local[d, 1].T
        rows[d, :width, :ndim] = left
        rows[d, :width, ndim:] = -right
        rows[d, width:, :ndim] = right
        rows[d, width:, ndim:] = left
        split[d] = local[d].astype(F32)

        def write(start, s, real, imag):
            top = slice(start, start + TILE)
            low = slice(nev + start, nev + start + TILE)
            at_r = slice(s * width, (s + 1) * width)
            at_i = slice((4 + s) * width, (5 + s) * width)
            mixed[d, top, at_r] = real.astype(BF)
            mixed[d, top, at_i] = imag.astype(BF)
            mixed[d, low, at_r] = imag.astype(BF)
            mixed[d, low, at_i] = (-real).astype(BF)

        steps = range(0, ndim, 2 * width)
        share = nev // len(steps)
        for turn, at in enumerate(steps):
            product = dot(rows[d], tau[:, at : at + 2 * width]).astype(BF)
            wide[d, :, at : at + 2 * width] = product[:width]
            wide[d, :, ndim + at : ndim + at + 2 * width] = product[width:]
            spin_mix(split.at[d], gamma, True, write, range(turn * share, (turn + 1) * share, TILE))
    scale = (2.0 * ndim) ** (-0.5)
    offset = DT - position[0]
    for k in range(out.shape[0]):
        first = lists[k, 0] + offset
        second = lists[k, 1] + offset
        spread = split.at[k % split.shape[0]]
        eigen_product(backward.at[lists[k, 2]], mixed.at[first], spread, width)
        u_r = spread[0].astype(BF)
        u_i = spread[1].astype(BF)
        pair = column.at[k % 2]
        pair[:ndim, :width] = u_r
        pair[:ndim, width:] = u_i
        pair[ndim:, :width] = u_i
        pair[ndim:, width:] = -u_r
        result = dot(wide[second], pair[...]) * scale
        result = jnp.where(k < count[0], result, 0.0)
        out[k, 0] = result[:, :width]
        out[k, 1] = result[:, width:]


def per_device(
    perambulator, elementals, sink_block, gamma_spin, graph_lists, diagram_counts, source_ids
):
    ndim, width = sink_block.shape[1:]
    slots = graph_lists.shape[1]
    nev = elementals.shape[3]
    row_block = lax.all_to_all(perambulator, "col", split_axis=1, concat_axis=1, tiled=True)
    pieces = row_block[0]
    chunks = 2 * pieces.shape[0]
    table = elementals[0]
    sink_t = jnp.swapaxes(sink_block, 1, 2)
    sink_rows = jnp.concatenate(
        [
            jnp.concatenate([sink_t[0], -sink_t[1]], axis=1),
            jnp.concatenate([sink_t[1], sink_t[0]], axis=1),
        ],
        axis=0,
    )
    forward = jnp.concatenate([table[:, 0], table[:, 1]], axis=2)
    backward = jnp.concatenate(
        [jnp.swapaxes(table[:, 0], 1, 2), jnp.swapaxes(table[:, 1], 1, 2)], axis=2
    )
    smem = pl.BlockSpec(memory_space=pltpu.SMEM)
    vmem = pl.BlockSpec(memory_space=pltpu.VMEM)
    free = pl.BlockSpec(memory_space=pl.ANY)
    dressed = pl.pallas_call(
        dress_kernel,
        out_shape=jax.ShapeDtypeStruct((2, ndim, width), BF),
        in_specs=[smem, smem, free, vmem, vmem],
        out_specs=vmem,
        scratch_shapes=[
            pltpu.VMEM((2 * ndim, ndim), BF),
            pltpu.VMEM((2, ndim, width), F32),
            pltpu.VMEM((2 * nev, 8 * width), BF),
            pltpu.SemaphoreType.DMA((chunks,)),
        ],
        compiler_params=pltpu.CompilerParams(vmem_limit_bytes=16 << 20),
        name="dress",
    )(source_ids, gamma_spin, pieces, sink_rows, forward)
    up = shifted(dressed, "src", 1)
    down = shifted(dressed, "src", -1)
    up, down = lax.optimization_barrier((up, down))
    up_two = shifted(up, "src", 1)
    down_two = shifted(down, "src", -1)
    position = lax.axis_index("src").astype(jnp.int32).reshape(1)
    reach = 2 * DT + 1
    totals = pl.pallas_call(
        diagrams_kernel,
        out_shape=jax.ShapeDtypeStruct((slots, 2, width, width), F32),
        in_specs=[smem] * 4 + [free] * 6 + [vmem],
        out_specs=vmem,
        scratch_shapes=[
            pltpu.VMEM((2 * ndim, ndim), BF),
            pltpu.VMEM((reach, width, 2 * ndim), BF),
            pltpu.VMEM((reach, 2 * nev, 8 * width), BF),
            pltpu.VMEM((reach, 2 * width, 2 * ndim), BF),
            pltpu.VMEM((reach, 2, ndim, width), F32),
            pltpu.VMEM((2, 2 * ndim, 2 * width), BF),
            pltpu.VMEM((reach, 2, ndim, width), BF),
            pltpu.SemaphoreType.DMA((chunks,)),
            pltpu.SemaphoreType.DMA((reach,)),
        ],
        compiler_params=pltpu.CompilerParams(vmem_limit_bytes=32 << 20),
        name="diagrams",
    )(
        graph_lists[0], diagram_counts, position, gamma_spin, pieces,
        up_two, up, dressed, down, down_two, backward,
    )
    return totals[None, None]


def solution(mesh):
    in_specs = (
        P("src", None, None, "col", None),
        P("col", None, None, None, None),
        P(),
        P(),
        P("src", None, None),
        P("src"),
        P("src"),
    )
    out_specs = P("src", "col", None, None, None, None)
    return jax.shard_map(
        per_device, mesh=mesh, in_specs=in_specs, out_specs=out_specs, check_vma=False
    )
```

```python
import functools

import jax
import jax.numpy as jnp
from jax import lax
from jax.experimental import pallas as pl
from jax.experimental.pallas import tpu as pltpu
from jax.sharding import PartitionSpec as P

DT = 2
TILE = 16
BF = jnp.bfloat16
F32 = jnp.float32


def swapped(shard, axis, start):
    count = lax.axis_size(axis)
    lower = range(start, count - 1, 2)
    return lax.ppermute(shard, axis, [(i, i + 1) for i in lower] + [(i + 1, i) for i in lower])


def dot(left, right):
    return jnp.dot(left, right, preferred_element_type=F32)


def stack_rows(real, imag, target, depth):
    width = real.shape[1]
    for at in range(0, real.shape[0], depth):
        upper = slice(2 * at, 2 * at + depth)
        lower = slice(2 * at + depth, 2 * at + 2 * depth)
        target[upper, :width] = real[at : at + depth]
        target[upper, width:] = imag[at : at + depth]
        target[lower, :width] = -imag[at : at + depth]
        target[lower, width:] = real[at : at + depth]


def spin_mix(split, gamma, adjoint, write, starts):
    for start in starts:
        part = [[split[c, pl.ds(4 * start + s, TILE, stride=4), :] for s in range(4)] for c in range(2)]
        for s in range(4):
            real = imag = None
            for q in range(4):
                if adjoint:
                    g_r, g_i = gamma[0, q, s], -gamma[1, q, s]
                else:
                    g_r, g_i = gamma[0, s, q], gamma[1, s, q]
                term_r = g_r * part[0][q] - g_i * part[1][q]
                term_i = g_r * part[1][q] + g_i * part[0][q]
                real = term_r if real is None else real + term_r
                imag = term_i if imag is None else imag + term_i
            write(start, s, real, imag)


def eigen_product(product, nev, split, width):
    for c in range(2):
        for half in range(2):
            at = (2 * c + half) * 2 * width
            done = product(slice(at, at + 2 * width))
            for q in range(2):
                split[c, pl.ds(2 * half + q, nev, stride=4), :] = done[:, q * width : (q + 1) * width]


def dress_kernel(ident, gamma, tau, sink, forward, out, split, mixed, matrix, rows, sem, *, depth):
    ndim, width = out.shape[1:]
    nev = ndim // 4
    fetch = pltpu.make_async_copy(forward.at[ident[0]], matrix, sem)
    fetch.start()
    stack_rows(sink[0], sink[1], rows, depth)
    left = rows[...].T
    for at in range(0, ndim, 2 * width):
        prop = dot(left, tau[:, at : at + 2 * width]).astype(BF).astype(F32)
        split[0, at : at + 2 * width, :] = prop[:width].T
        split[1, at : at + 2 * width, :] = prop[width:].T

    def write(start, s, real, imag):
        rows = slice(start, start + TILE)
        low = slice(nev + start, nev + start + TILE)
        at_r = slice(s * width, (s + 1) * width)
        at_i = slice((4 + s) * width, (5 + s) * width)
        mixed[rows, at_r] = real.astype(BF)
        mixed[rows, at_i] = imag.astype(BF)
        mixed[low, at_r] = (-imag).astype(BF)
        mixed[low, at_i] = real.astype(BF)

    spin_mix(split, gamma, False, write, range(0, nev, TILE))
    fetch.wait()

    def product(at):
        return dot(matrix[0], mixed[:nev, at]) + dot(matrix[1], mixed[nev:, at])

    eigen_product(product, nev, split, width)
    out[...] = split[...].astype(BF)


def prepare(d, block, gamma, tau, wide, mixed, rows, split, depth):
    ndim, width = block.shape[1:]
    nev = ndim // 4
    split[...] = block[...].astype(F32)

    def write(start, s, real, imag):
        top = slice(start, start + TILE)
        low = slice(nev + start, nev + start + TILE)
        at_r = slice(s * width, (s + 1) * width)
        at_i = slice((4 + s) * width, (5 + s) * width)
        mixed[d, top, at_r] = real.astype(BF)
        mixed[d, top, at_i] = imag.astype(BF)
        mixed[d, low, at_r] = imag.astype(BF)
        mixed[d, low, at_i] = (-real).astype(BF)

    spin_mix(split, gamma, True, write, range(0, nev, TILE))
    stack_rows(block[0], block[1], rows, depth)
    left = rows[...].T
    for at in range(0, ndim, 2 * width):
        product = dot(left, tau[:, at : at + 2 * width]).astype(BF)
        wide[d, :, at : at + 2 * width] = product[:width]
        wide[d, :, ndim + at : ndim + at + 2 * width] = product[width:]


def prepare_kernel(*refs, depth, entries, fresh):
    gamma, tau = refs[:2]
    blocks = refs[2 : 2 + len(entries)]
    rest = refs[2 + len(entries) + (0 if fresh else 2) :]
    wide, mixed, rows, split = rest
    for turn, (d, block) in enumerate(zip(entries, blocks)):
        prepare(d, block, gamma, tau, wide, mixed, rows.at[turn], split.at[turn], depth)


def diagrams_kernel(
    lists, count, position, gamma, tau, low, high, backward, wide_in, mixed_in, out, wide, mixed,
    rows, split, column, *, depth,
):
    ndim, width = low.shape[1:]
    nev = ndim // 4
    prepare(3, low, gamma, tau, wide, mixed, rows.at[0], split.at[0], depth)
    prepare(4, high, gamma, tau, wide, mixed, rows.at[1], split.at[1], depth)
    scale = (2.0 * ndim) ** (-0.5)
    here = position[0]
    sign = 1 - 2 * (here % 2)

    def entry(sender):
        ahead = (sender - here) * sign
        near = jnp.where(ahead == 1, 1, 2)
        far = jnp.where(ahead == 2, 3, 4)
        return jnp.where(ahead == 0, 0, jnp.where(ahead * ahead == 1, near, far))

    for k in range(out.shape[0]):
        first = entry(lists[k, 0])
        second = entry(lists[k, 1])
        spread = split.at[k % 2]

        def product(at):
            return dot(backward[lists[k, 2]], mixed[first, :, at])

        eigen_product(product, nev, spread, width)
        u_r = spread[0].astype(BF)
        u_i = spread[1].astype(BF)
        pair = column.at[k % 2]
        pair[:ndim, :width] = u_r
        pair[:ndim, width:] = u_i
        pair[ndim:, :width] = u_i
        pair[ndim:, width:] = -u_r
        result = dot(wide[second], pair[...]) * scale
        result = jnp.where(k < count[0], result, 0.0)
        out[k, 0] = result[:, :width]
        out[k, 1] = result[:, width:]


def per_device(
    perambulator, elementals, sink_block, gamma_spin, graph_lists, diagram_counts, source_ids
):
    ndim, width = sink_block.shape[1:]
    slots = graph_lists.shape[1]
    nev = elementals.shape[3]
    depth = perambulator.shape[3]
    reach = 2 * DT + 1
    row_block = lax.all_to_all(perambulator, "col", split_axis=1, concat_axis=1, tiled=True)
    tau = row_block.reshape(2 * ndim, ndim)
    table = elementals[0]
    backward = jnp.concatenate(
        [jnp.swapaxes(table[:, 0], 1, 2), jnp.swapaxes(table[:, 1], 1, 2)], axis=2
    )
    tau, backward = lax.optimization_barrier((tau, backward))
    smem = pl.BlockSpec(memory_space=pltpu.SMEM)
    vmem = pl.BlockSpec(memory_space=pltpu.VMEM)
    free = pl.BlockSpec(memory_space=pl.ANY)

    def scratch(count):
        return [
            pltpu.VMEM((count, 2 * ndim, 2 * width), BF),
            pltpu.VMEM((2, 2, ndim, width), F32),
        ]

    dressed = pl.pallas_call(
        functools.partial(dress_kernel, depth=depth),
        out_shape=jax.ShapeDtypeStruct((2, ndim, width), BF),
        in_specs=[smem, smem, vmem, vmem, free],
        out_specs=vmem,
        scratch_shapes=[
            pltpu.VMEM((2, ndim, width), F32),
            pltpu.VMEM((2 * nev, 8 * width), BF),
            pltpu.VMEM((2, nev, nev), BF),
            pltpu.VMEM((2 * ndim, 2 * width), BF),
            pltpu.SemaphoreType.DMA,
        ],
        compiler_params=pltpu.CompilerParams(vmem_limit_bytes=10 << 20),
        name="dress",
    )(source_ids, gamma_spin, tau, sink_block, table)
    state = (
        jax.ShapeDtypeStruct((reach, width, 2 * ndim), BF),
        jax.ShapeDtypeStruct((reach, 2 * nev, 8 * width), BF),
    )

    def prepared(blocks, entries, held=()):
        fresh = not held
        count = 2 + len(blocks)
        return pl.pallas_call(
            functools.partial(prepare_kernel, depth=depth, entries=entries, fresh=fresh),
            out_shape=state,
            in_specs=[smem, vmem] + [vmem] * (len(blocks) + len(held)),
            out_specs=(vmem, vmem),
            scratch_shapes=scratch(len(blocks)),
            input_output_aliases={} if fresh else {count: 0, count + 1: 1},
            compiler_params=pltpu.CompilerParams(vmem_limit_bytes=12 << 20),
            name="prepare",
        )(gamma_spin, tau, *blocks, *held)

    even = swapped(dressed, "src", 0)
    odd = swapped(dressed, "src", 1)
    held = prepared((dressed,), (0,))
    odd_far = swapped(even, "src", 1)
    even_far = swapped(odd, "src", 0)
    held = prepared((even, odd), (1, 2), held)
    position = lax.axis_index("src").astype(jnp.int32).reshape(1)
    totals, _, _ = pl.pallas_call(
        functools.partial(diagrams_kernel, depth=depth),
        out_shape=(jax.ShapeDtypeStruct((slots, 2, width, width), F32), *state),
        in_specs=[smem] * 4 + [vmem] * 6,
        out_specs=(vmem, vmem, vmem),
        scratch_shapes=scratch(2) + [pltpu.VMEM((2, 2 * ndim, 2 * width), BF)],
        input_output_aliases={8: 1, 9: 2},
        compiler_params=pltpu.CompilerParams(vmem_limit_bytes=16 << 20),
        name="diagrams",
    )(
        graph_lists[0], diagram_counts, position, gamma_spin, tau, even_far, odd_far, backward, *held
    )
    return totals[None, None]


def solution(mesh):
    in_specs = (
        P("src", None, None, "col", None),
        P("col", None, None, None, None),
        P(),
        P(),
        P("src", None, None),
        P("src"),
        P("src"),
    )
    out_specs = P("src", "col", None, None, None, None)
    return jax.shard_map(
        per_device, mesh=mesh, in_specs=in_specs, out_specs=out_specs, check_vma=False
    )
```

```python
import functools

import jax
import jax.numpy as jnp
from jax import lax
from jax.experimental import pallas as pl
from jax.experimental.pallas import tpu as pltpu
from jax.sharding import PartitionSpec as P

DT = 2
TILE = 16
BF = jnp.bfloat16
F32 = jnp.float32


def swapped(shard, axis, start):
    count = lax.axis_size(axis)
    lower = range(start, count - 1, 2)
    return lax.ppermute(shard, axis, [(i, i + 1) for i in lower] + [(i + 1, i) for i in lower])


def dot(left, right):
    return jnp.dot(left, right, preferred_element_type=F32)


def stack_rows(real, imag, target, depth):
    width = real.shape[1]
    for at in range(0, real.shape[0], depth):
        upper = slice(2 * at, 2 * at + depth)
        lower = slice(2 * at + depth, 2 * at + 2 * depth)
        target[upper, :width] = real[at : at + depth]
        target[upper, width:] = imag[at : at + depth]
        target[lower, :width] = -imag[at : at + depth]
        target[lower, width:] = real[at : at + depth]


def spin_mix(split, gamma, adjoint, write, starts):
    for start in starts:
        part = [[split[c, pl.ds(4 * start + s, TILE, stride=4), :] for s in range(4)] for c in range(2)]
        for s in range(4):
            real = imag = None
            for q in range(4):
                if adjoint:
                    g_r, g_i = gamma[0, q, s], -gamma[1, q, s]
                else:
                    g_r, g_i = gamma[0, s, q], gamma[1, s, q]
                term_r = g_r * part[0][q] - g_i * part[1][q]
                term_i = g_r * part[1][q] + g_i * part[0][q]
                real = term_r if real is None else real + term_r
                imag = term_i if imag is None else imag + term_i
            write(start, s, real, imag)


def eigen_product(product, nev, split, width):
    for c in range(2):
        for half in range(2):
            at = (2 * c + half) * 2 * width
            done = product(slice(at, at + 2 * width))
            for q in range(2):
                split[c, pl.ds(2 * half + q, nev, stride=4), :] = done[:, q * width : (q + 1) * width]


def left_kernel(sink, left, rows, *, depth):
    stack_rows(sink[0], sink[1], rows, depth)
    left[...] = rows[...].T


def dress_kernel(ident, gamma, tau, left, table, out, split, mixed, matrix, sem):
    ndim, width = out.shape[1:]
    nev = ndim // 4
    fetch = pltpu.make_async_copy(table.at[ident[0]], matrix, sem)
    fetch.start()
    for at in range(0, ndim, 2 * width):
        prop = dot(left[...], tau[:, at : at + 2 * width]).astype(BF).astype(F32)
        split[0, at : at + 2 * width, :] = prop[:width].T
        split[1, at : at + 2 * width, :] = prop[width:].T

    def write(start, s, real, imag):
        rows = slice(start, start + TILE)
        low = slice(nev + start, nev + start + TILE)
        at_r = slice(s * width, (s + 1) * width)
        at_i = slice((4 + s) * width, (5 + s) * width)
        mixed[rows, at_r] = real.astype(BF)
        mixed[rows, at_i] = imag.astype(BF)
        mixed[low, at_r] = (-imag).astype(BF)
        mixed[low, at_i] = real.astype(BF)

    spin_mix(split, gamma, False, write, range(0, nev, TILE))
    fetch.wait()

    def product(at):
        return dot(matrix[0], mixed[:nev, at]) + dot(matrix[1], mixed[nev:, at])

    eigen_product(product, nev, split, width)
    out[...] = split[...].astype(BF)


def prepare(d, block, gamma, tau, wide, mixed, rows, split, depth):
    ndim, width = block.shape[1:]
    nev = ndim // 4
    split[...] = block[...].astype(F32)

    def write(start, s, real, imag):
        top = slice(start, start + TILE)
        low = slice(nev + start, nev + start + TILE)
        at_r = slice(s * width, (s + 1) * width)
        at_i = slice((4 + s) * width, (5 + s) * width)
        mixed[d, top, at_r] = real.astype(BF)
        mixed[d, top, at_i] = imag.astype(BF)
        mixed[d, low, at_r] = imag.astype(BF)
        mixed[d, low, at_i] = (-real).astype(BF)

    spin_mix(split, gamma, True, write, range(0, nev, TILE))
    stack_rows(block[0], block[1], rows, depth)
    left = rows[...].T
    for at in range(0, ndim, 2 * width):
        product = dot(left, tau[:, at : at + 2 * width]).astype(BF)
        wide[d, :, at : at + 2 * width] = product[:width]
        wide[d, :, ndim + at : ndim + at + 2 * width] = product[width:]


def sort_kernel(tau, _, sorted_tau, order, chunk):
    ndim = tau.shape[1]
    nev = ndim // 4
    row = lax.broadcasted_iota(jnp.int32, (ndim, nev), 0)
    column = lax.broadcasted_iota(jnp.int32, (ndim, nev), 1)
    for s in range(4):
        order[:, s * nev : (s + 1) * nev] = (row == 4 * column + s).astype(F32).astype(BF)
    for turn, at in enumerate(range(0, 2 * ndim, 256)):
        chunk[turn % 2] = tau[at : at + 256, :]
        sorted_tau[at : at + 256, :] = dot(chunk[turn % 2], order[...]).astype(BF)


def own_kernel(gamma, tau, block, table, wide, mixed, fetched, rows, split, sem, *, depth):
    fetch = pltpu.make_async_copy(table, fetched, sem)
    fetch.start()
    prepare(0, block, gamma, tau, wide, mixed, rows, split, depth)
    fetch.wait()


def prepare_kernel(*refs, depth, entries):
    gamma, tau = refs[:2]
    blocks = refs[2 : 2 + len(entries)]
    wide, mixed, rows, split = refs[2 + len(entries) + 2 :]
    for turn, (d, block) in enumerate(zip(entries, blocks)):
        prepare(d, block, gamma, tau, wide, mixed, rows.at[turn], split.at[turn], depth)


def diagrams_kernel(
    lists, count, position, gamma, tau, last, backward, wide_in, mixed_in, out, wide, mixed,
    rows, split, column, totals, sem, *, depth,
):
    ndim, width = last.shape[1:]
    nev = ndim // 4
    prepare(3, last, gamma, tau, wide, mixed, rows, split, depth)
    scale = (2.0 * ndim) ** (-0.5)
    here = position[0]
    sign = 1 - 2 * (here % 2)

    def entry(sender):
        ahead = (sender - here) * sign
        near = jnp.where(ahead == 1, 1, 2)
        far = jnp.where(ahead == 2, 3, 4)
        return jnp.where(ahead == 0, 0, jnp.where(ahead * ahead == 1, near, far))

    for k in range(out.shape[0]):
        first = entry(lists[k, 0])
        second = entry(lists[k, 1])
        pair = column.at[k % 2]
        for half in range(2):
            at = 2 * half * width
            real = dot(backward[lists[k, 2]], mixed[first, :, at : at + 2 * width]).astype(BF)
            at += 4 * width
            imag = dot(backward[lists[k, 2]], mixed[first, :, at : at + 2 * width]).astype(BF)
            for q in range(2):
                s = 2 * half + q
                part = slice(q * width, (q + 1) * width)
                top = slice(s * nev, (s + 1) * nev)
                low = slice(ndim + s * nev, ndim + (s + 1) * nev)
                pair[top, :width] = real[:, part]
                pair[top, width:] = imag[:, part]
                pair[low, :width] = imag[:, part]
                pair[low, width:] = -real[:, part]
        result = dot(wide[second], pair[...]) * scale
        result = jnp.where(k < count[0], result, 0.0)
        totals[k, 0] = result[:, :width]
        totals[k, 1] = result[:, width:]
        pltpu.make_async_copy(totals.at[k], out.at[k], sem.at[k]).start()
    for k in range(out.shape[0]):
        pltpu.make_async_copy(totals.at[k], out.at[k], sem.at[k]).wait()


def per_device(
    perambulator, elementals, sink_block, gamma_spin, graph_lists, diagram_counts, source_ids
):
    ndim, width = sink_block.shape[1:]
    slots = graph_lists.shape[1]
    nev = elementals.shape[3]
    depth = perambulator.shape[3]
    reach = 2 * DT + 1
    row_block = lax.all_to_all(perambulator, "col", split_axis=1, concat_axis=1, tiled=True)
    tau = row_block.reshape(2 * ndim, ndim)
    table = elementals[0]
    backward = jnp.concatenate(
        [jnp.swapaxes(table[:, 0], 1, 2), jnp.swapaxes(table[:, 1], 1, 2)], axis=2
    )
    smem = pl.BlockSpec(memory_space=pltpu.SMEM)
    vmem = pl.BlockSpec(memory_space=pltpu.VMEM)
    free = pl.BlockSpec(memory_space=pl.ANY)
    rows = pltpu.VMEM((2 * ndim, 2 * width), BF)
    split = pltpu.VMEM((2, ndim, width), F32)
    left = pl.pallas_call(
        functools.partial(left_kernel, depth=depth),
        out_shape=jax.ShapeDtypeStruct((2 * width, 2 * ndim), BF),
        in_specs=[vmem],
        out_specs=vmem,
        scratch_shapes=[rows],
        compiler_params=pltpu.CompilerParams(vmem_limit_bytes=6 << 20),
        name="left",
    )(sink_block)
    tau, backward, left = lax.optimization_barrier((tau, backward, left))
    backward = pltpu.with_memory_space_constraint(backward, pltpu.HBM)

    dressed = pl.pallas_call(
        dress_kernel,
        out_shape=jax.ShapeDtypeStruct((2, ndim, width), BF),
        in_specs=[smem, smem, vmem, vmem, free],
        out_specs=vmem,
        scratch_shapes=[
            pltpu.VMEM((2, ndim, width), F32),
            pltpu.VMEM((2 * nev, 8 * width), BF),
            pltpu.VMEM((2, nev, nev), BF),
            pltpu.SemaphoreType.DMA,
        ],
        compiler_params=pltpu.CompilerParams(vmem_limit_bytes=10 << 20),
        name="dress",
    )(source_ids, gamma_spin, tau, left, pltpu.with_memory_space_constraint(table, pltpu.HBM))
    state = (
        jax.ShapeDtypeStruct((reach, width, 2 * ndim), BF),
        jax.ShapeDtypeStruct((reach, 2 * nev, 8 * width), BF),
    )


    def prepared(blocks, entries, held):
        count = 2 + len(blocks)
        return pl.pallas_call(
            functools.partial(prepare_kernel, depth=depth, entries=entries),
            out_shape=state,
            in_specs=[smem, vmem] + [vmem] * (len(blocks) + len(held)),
            out_specs=(vmem, vmem),
            scratch_shapes=[
                pltpu.VMEM((len(blocks), *rows.shape), BF),
                pltpu.VMEM((len(blocks), *split.shape), F32),
            ],
            input_output_aliases={count: 0, count + 1: 1},
            compiler_params=pltpu.CompilerParams(vmem_limit_bytes=12 << 20),
            name="prepare",
        )(gamma_spin, tau, *blocks, *held)

    even = swapped(dressed, "src", 0)
    odd = swapped(dressed, "src", 1)
    tau = pl.pallas_call(
        sort_kernel,
        out_shape=jax.ShapeDtypeStruct(tau.shape, BF),
        in_specs=[vmem, free],
        out_specs=vmem,
        scratch_shapes=[pltpu.VMEM((ndim, ndim), BF), pltpu.VMEM((2, 256, ndim), BF)],
        compiler_params=pltpu.CompilerParams(vmem_limit_bytes=8 << 20),
        input_output_aliases={0: 0},
        name="sort",
    )(tau, dressed)
    even, tau = lax.optimization_barrier((even, tau))
    odd_far = swapped(even, "src", 1)
    even_far = swapped(odd, "src", 0)
    *held, backward = pl.pallas_call(
        functools.partial(own_kernel, depth=depth),
        out_shape=(*state, jax.ShapeDtypeStruct(backward.shape, BF)),
        in_specs=[smem, vmem, vmem, free],
        out_specs=(vmem, vmem, vmem),
        scratch_shapes=[rows, split, pltpu.SemaphoreType.DMA],
        compiler_params=pltpu.CompilerParams(vmem_limit_bytes=12 << 20),
        name="own",
    )(gamma_spin, tau, dressed, backward)
    held = prepared((even, odd), (1, 2), held)
    held = prepared((odd_far,), (4,), held)
    position = lax.axis_index("src").astype(jnp.int32).reshape(1)
    totals, _, _ = pl.pallas_call(
        functools.partial(diagrams_kernel, depth=depth),
        out_shape=(jax.ShapeDtypeStruct((slots, 2, width, width), F32), *state),
        in_specs=[smem] * 4 + [vmem] * 5,
        out_specs=(free, vmem, vmem),
        scratch_shapes=[
            rows,
            split,
            pltpu.VMEM((2, 2 * ndim, 2 * width), BF),
            pltpu.VMEM((slots, 2, width, width), F32),
            pltpu.SemaphoreType.DMA((slots,)),
        ],
        input_output_aliases={7: 1, 8: 2},
        compiler_params=pltpu.CompilerParams(vmem_limit_bytes=16 << 20),
        name="diagrams",
    )(
        graph_lists[0], diagram_counts, position, gamma_spin, tau, even_far, backward, *held
    )
    return totals[None, None]


def solution(mesh):
    in_specs = (
        P("src", None, None, "col", None),
        P("col", None, None, None, None),
        P(),
        P(),
        P("src", None, None),
        P("src"),
        P("src"),
    )
    out_specs = P("src", "col", None, None, None, None)
    return jax.shard_map(
        per_device, mesh=mesh, in_specs=in_specs, out_specs=out_specs, check_vma=False
    )
```

```python
import functools

import jax
import jax.numpy as jnp
from jax import lax
from jax.experimental import pallas as pl
from jax.experimental.pallas import tpu as pltpu
from jax.sharding import PartitionSpec as P

DT = 2
TILE = 16
BF = jnp.bfloat16
F32 = jnp.float32


def swapped(shard, axis, start):
    count = lax.axis_size(axis)
    lower = range(start, count - 1, 2)
    return lax.ppermute(shard, axis, [(i, i + 1) for i in lower] + [(i + 1, i) for i in lower])


def dot(left, right):
    return jnp.dot(left, right, preferred_element_type=F32)


def stack_rows(real, imag, target, depth):
    width = real.shape[1]
    for at in range(0, real.shape[0], depth):
        upper = slice(2 * at, 2 * at + depth)
        lower = slice(2 * at + depth, 2 * at + 2 * depth)
        target[upper, :width] = real[at : at + depth]
        target[upper, width:] = imag[at : at + depth]
        target[lower, :width] = -imag[at : at + depth]
        target[lower, width:] = real[at : at + depth]


def spin_mix(split, gamma, adjoint, write, starts):
    for start in starts:
        part = [[split[c, pl.ds(4 * start + s, TILE, stride=4), :] for s in range(4)] for c in range(2)]
        for s in range(4):
            real = imag = None
            for q in range(4):
                at = 4 * q + s if adjoint else 4 * s + q
                g_r = gamma[pl.ds(at, TILE, stride=0), :]
                g_i = gamma[pl.ds(16 + at, TILE, stride=0), :]
                cross_r = g_i * part[1][q]
                cross_i = g_i * part[0][q]
                term_r = g_r * part[0][q] + cross_r if adjoint else g_r * part[0][q] - cross_r
                term_i = g_r * part[1][q] - cross_i if adjoint else g_r * part[1][q] + cross_i
                real = term_r if real is None else real + term_r
                imag = term_i if imag is None else imag + term_i
            write(start, s, real, imag)


def eigen_product(product, nev, split, width):
    for c in range(2):
        for half in range(2):
            at = (2 * c + half) * 2 * width
            done = product(slice(at, at + 2 * width))
            for q in range(2):
                split[c, pl.ds(2 * half + q, nev, stride=4), :] = done[:, q * width : (q + 1) * width]


def left_kernel(ident, sink, table, left, rows, *, depth):
    nev = table.shape[3]
    stack_rows(sink[0], sink[1], rows, depth)
    left[:, : rows.shape[0]] = rows[...].T
    for c in range(2):
        at = rows.shape[0] + c * 256
        left[:nev, at : at + nev] = table[ident[0], c]


def dress_kernel(gamma, tau, left, out, split, mixed):
    ndim, width = out.shape[1:]
    nev = ndim // 4
    for at in range(0, ndim, 2 * width):
        prop = dot(left[:, : 2 * ndim], tau[:, at : at + 2 * width]).astype(BF).astype(F32)
        split[0, at : at + 2 * width, :] = prop[:width].T
        split[1, at : at + 2 * width, :] = prop[width:].T

    def write(start, s, real, imag):
        rows = slice(start, start + TILE)
        low = slice(nev + start, nev + start + TILE)
        at_r = slice(s * width, (s + 1) * width)
        at_i = slice((4 + s) * width, (5 + s) * width)
        mixed[rows, at_r] = real.astype(BF)
        mixed[rows, at_i] = imag.astype(BF)
        mixed[low, at_r] = (-imag).astype(BF)
        mixed[low, at_i] = real.astype(BF)

    spin_mix(split, gamma, False, write, range(0, nev, TILE))
    real = left[:nev, 2 * ndim : 2 * ndim + nev]
    imag = left[:nev, 2 * ndim + 256 : 2 * ndim + 256 + nev]

    def product(at):
        return dot(real, mixed[:nev, at]) + dot(imag, mixed[nev:, at])

    eigen_product(product, nev, split, width)
    out[...] = split[...].astype(BF)


def prepare(d, block, gamma, tau, wide, mixed, rows, split, depth):
    ndim, width = block.shape[1:]
    nev = ndim // 4
    split[...] = block[...].astype(F32)

    def write(start, s, real, imag):
        top = slice(start, start + TILE)
        low = slice(nev + start, nev + start + TILE)
        at_r = slice(s * width, (s + 1) * width)
        at_i = slice((4 + s) * width, (5 + s) * width)
        mixed[d, top, at_r] = real.astype(BF)
        mixed[d, top, at_i] = imag.astype(BF)
        mixed[d, low, at_r] = imag.astype(BF)
        mixed[d, low, at_i] = (-real).astype(BF)

    spin_mix(split, gamma, True, write, range(0, nev, TILE))
    stack_rows(block[0], block[1], rows, depth)
    left = rows[...].T
    for at in range(0, ndim, 2 * width):
        product = dot(left, tau[:, at : at + 2 * width]).astype(BF)
        wide[d, :, at : at + 2 * width] = product[:width]
        wide[d, :, ndim + at : ndim + at + 2 * width] = product[width:]


def sort_kernel(tau, _, sorted_tau, order, chunk):
    ndim = tau.shape[1]
    nev = ndim // 4
    row = lax.broadcasted_iota(jnp.int32, (ndim, nev), 0)
    column = lax.broadcasted_iota(jnp.int32, (ndim, nev), 1)
    for s in range(4):
        order[:, s * nev : (s + 1) * nev] = (row == 4 * column + s).astype(F32).astype(BF)
    for turn, at in enumerate(range(0, 2 * ndim, 256)):
        chunk[turn % 2] = tau[at : at + 256, :]
        sorted_tau[at : at + 256, :] = dot(chunk[turn % 2], order[...]).astype(BF)


def own_kernel(gamma, tau, block, table, wide, mixed, fetched, rows, split, sem, *, depth):
    fetch = pltpu.make_async_copy(table, fetched, sem)
    fetch.start()
    prepare(0, block, gamma, tau, wide, mixed, rows, split, depth)
    fetch.wait()


def prepare_kernel(*refs, depth, entries):
    gamma, tau = refs[:2]
    blocks = refs[2 : 2 + len(entries)]
    wide, mixed, rows, split = refs[2 + len(entries) + 2 :]
    for turn, (d, block) in enumerate(zip(entries, blocks)):
        prepare(d, block, gamma, tau, wide, mixed, rows.at[turn], split.at[turn], depth)


def diagrams_kernel(
    meta, gamma, tau, last, backward, wide_in, mixed_in, out, wide, mixed,
    rows, split, column, totals, sem, *, depth,
):
    ndim, width = last.shape[1:]
    nev = ndim // 4
    prepare(3, last, gamma, tau, wide, mixed, rows, split, depth)
    scale = (2.0 * ndim) ** (-0.5)
    here = meta[meta.shape[0] - 1]
    sign = 1 - 2 * (here % 2)

    def entry(sender):
        ahead = (sender - here) * sign
        near = jnp.where(ahead == 1, 1, 2)
        far = jnp.where(ahead == 2, 3, 4)
        return jnp.where(ahead == 0, 0, jnp.where(ahead * ahead == 1, near, far))

    for k in range(out.shape[0]):
        first = entry(meta[3 * k])
        second = entry(meta[3 * k + 1])
        pair = column.at[k % 2]
        for half in range(2):
            at = 2 * half * width
            real = dot(backward[meta[3 * k + 2]], mixed[first, :, at : at + 2 * width]).astype(BF)
            at += 4 * width
            imag = dot(backward[meta[3 * k + 2]], mixed[first, :, at : at + 2 * width]).astype(BF)
            for q in range(2):
                s = 2 * half + q
                part = slice(q * width, (q + 1) * width)
                top = slice(s * nev, (s + 1) * nev)
                low = slice(ndim + s * nev, ndim + (s + 1) * nev)
                pair[top, :width] = real[:, part]
                pair[top, width:] = imag[:, part]
                pair[low, :width] = imag[:, part]
                pair[low, width:] = -real[:, part]
        result = dot(wide[second], pair[...]) * scale
        result = jnp.where(k < meta[meta.shape[0] - 2], result, 0.0)
        totals[k, 0] = result[:, :width]
        totals[k, 1] = result[:, width:]
        pltpu.make_async_copy(totals.at[k], out.at[k], sem.at[k]).start()
    for k in range(out.shape[0]):
        pltpu.make_async_copy(totals.at[k], out.at[k], sem.at[k]).wait()


def per_device(
    perambulator, elementals, sink_block, gamma_spin, graph_lists, diagram_counts, source_ids
):
    ndim, width = sink_block.shape[1:]
    slots = graph_lists.shape[1]
    nev = elementals.shape[3]
    depth = perambulator.shape[3]
    reach = 2 * DT + 1
    row_block = lax.all_to_all(perambulator, "col", split_axis=1, concat_axis=1, tiled=True)
    tau = row_block.reshape(2 * ndim, ndim)
    table = elementals[0]
    backward = jnp.concatenate(
        [jnp.swapaxes(table[:, 0], 1, 2), jnp.swapaxes(table[:, 1], 1, 2)], axis=2
    )
    smem = pl.BlockSpec(memory_space=pltpu.SMEM)
    vmem = pl.BlockSpec(memory_space=pltpu.VMEM)
    free = pl.BlockSpec(memory_space=pl.ANY)
    rows = pltpu.VMEM((2 * ndim, 2 * width), BF)
    split = pltpu.VMEM((2, ndim, width), F32)
    left = pl.pallas_call(
        functools.partial(left_kernel, depth=depth),
        out_shape=jax.ShapeDtypeStruct((2 * width, 2 * ndim + 512), BF),
        in_specs=[smem, vmem, vmem],
        out_specs=vmem,
        scratch_shapes=[rows],
        compiler_params=pltpu.CompilerParams(vmem_limit_bytes=8 << 20),
        name="left",
    )(source_ids, sink_block, table)
    gamma = jnp.broadcast_to(gamma_spin.reshape(-1, 1), (gamma_spin.size, width))
    position = lax.axis_index("src").astype(jnp.int32).reshape(1)
    meta = jnp.concatenate([graph_lists.reshape(-1), diagram_counts, position])
    tau, backward, left, gamma, meta = lax.optimization_barrier((tau, backward, left, gamma, meta))
    backward = pltpu.with_memory_space_constraint(backward, pltpu.HBM)

    dressed = pl.pallas_call(
        dress_kernel,
        out_shape=jax.ShapeDtypeStruct((2, ndim, width), BF),
        in_specs=[vmem, vmem, vmem],
        out_specs=vmem,
        scratch_shapes=[
            pltpu.VMEM((2, ndim, width), F32),
            pltpu.VMEM((2 * nev, 8 * width), BF),
        ],
        compiler_params=pltpu.CompilerParams(vmem_limit_bytes=10 << 20),
        name="dress",
    )(gamma, tau, left)
    state = (
        jax.ShapeDtypeStruct((reach, width, 2 * ndim), BF),
        jax.ShapeDtypeStruct((reach, 2 * nev, 8 * width), BF),
    )


    def prepared(blocks, entries, held):
        count = 2 + len(blocks)
        return pl.pallas_call(
            functools.partial(prepare_kernel, depth=depth, entries=entries),
            out_shape=state,
            in_specs=[vmem] * (2 + len(blocks) + len(held)),
            out_specs=(vmem, vmem),
            scratch_shapes=[
                pltpu.VMEM((len(blocks), *rows.shape), BF),
                pltpu.VMEM((len(blocks), *split.shape), F32),
            ],
            input_output_aliases={count: 0, count + 1: 1},
            compiler_params=pltpu.CompilerParams(vmem_limit_bytes=12 << 20),
            name="prepare",
        )(gamma, tau, *blocks, *held)

    even = swapped(dressed, "src", 0)
    odd = swapped(dressed, "src", 1)
    tau = pl.pallas_call(
        sort_kernel,
        out_shape=jax.ShapeDtypeStruct(tau.shape, BF),
        in_specs=[vmem, free],
        out_specs=vmem,
        scratch_shapes=[pltpu.VMEM((ndim, ndim), BF), pltpu.VMEM((2, 256, ndim), BF)],
        compiler_params=pltpu.CompilerParams(vmem_limit_bytes=8 << 20),
        input_output_aliases={0: 0},
        name="sort",
    )(tau, dressed)
    even, tau = lax.optimization_barrier((even, tau))
    odd_far = swapped(even, "src", 1)
    even_far = swapped(odd, "src", 0)
    *held, backward = pl.pallas_call(
        functools.partial(own_kernel, depth=depth),
        out_shape=(*state, jax.ShapeDtypeStruct(backward.shape, BF)),
        in_specs=[vmem, vmem, vmem, free],
        out_specs=(vmem, vmem, vmem),
        scratch_shapes=[rows, split, pltpu.SemaphoreType.DMA],
        compiler_params=pltpu.CompilerParams(vmem_limit_bytes=12 << 20),
        name="own",
    )(gamma, tau, dressed, backward)
    held = prepared((even, odd), (1, 2), held)
    held = prepared((odd_far,), (4,), held)
    totals, _, _ = pl.pallas_call(
        functools.partial(diagrams_kernel, depth=depth),
        out_shape=(jax.ShapeDtypeStruct((slots, 2, width, width), F32), *state),
        in_specs=[smem] + [vmem] * 6,
        out_specs=(free, vmem, vmem),
        scratch_shapes=[
            rows,
            split,
            pltpu.VMEM((2, 2 * ndim, 2 * width), BF),
            pltpu.VMEM((slots, 2, width, width), F32),
            pltpu.SemaphoreType.DMA((slots,)),
        ],
        input_output_aliases={5: 1, 6: 2},
        compiler_params=pltpu.CompilerParams(vmem_limit_bytes=16 << 20),
        name="diagrams",
    )(
        meta, gamma, tau, even_far, backward, *held
    )
    return totals[None, None]


def solution(mesh):
    in_specs = (
        P("src", None, None, "col", None),
        P("col", None, None, None, None),
        P(),
        P(),
        P("src", None, None),
        P("src"),
        P("src"),
    )
    out_specs = P("src", "col", None, None, None, None)
    return jax.shard_map(
        per_device, mesh=mesh, in_specs=in_specs, out_specs=out_specs, check_vma=False
    )
```

```python
import functools

import jax
import jax.numpy as jnp
from jax import lax
from jax.experimental import pallas as pl
from jax.experimental.pallas import tpu as pltpu
from jax.sharding import PartitionSpec as P

DT = 2
TILE = 16
SURE = 2
BF = jnp.bfloat16
F32 = jnp.float32


def swapped(shard, axis, start):
    count = lax.axis_size(axis)
    lower = range(start, count - 1, 2)
    return lax.ppermute(shard, axis, [(i, i + 1) for i in lower] + [(i + 1, i) for i in lower])


def dot(left, right):
    return jnp.dot(left, right, preferred_element_type=F32)


def stack_rows(real, imag, target, depth):
    width = real.shape[1]
    for at in range(0, real.shape[0], depth):
        upper = slice(2 * at, 2 * at + depth)
        lower = slice(2 * at + depth, 2 * at + 2 * depth)
        target[upper, :width] = real[at : at + depth]
        target[upper, width:] = imag[at : at + depth]
        target[lower, :width] = -imag[at : at + depth]
        target[lower, width:] = real[at : at + depth]


def spin_mix(split, gamma, adjoint, write, starts):
    for start in starts:
        part = [[split[c, pl.ds(4 * start + s, TILE, stride=4), :] for s in range(4)] for c in range(2)]
        for s in range(4):
            real = imag = None
            for q in range(4):
                at = 4 * q + s if adjoint else 4 * s + q
                g_r = gamma[pl.ds(at, TILE, stride=0), :]
                g_i = gamma[pl.ds(16 + at, TILE, stride=0), :]
                cross_r = g_i * part[1][q]
                cross_i = g_i * part[0][q]
                term_r = g_r * part[0][q] + cross_r if adjoint else g_r * part[0][q] - cross_r
                term_i = g_r * part[1][q] - cross_i if adjoint else g_r * part[1][q] + cross_i
                real = term_r if real is None else real + term_r
                imag = term_i if imag is None else imag + term_i
            write(start, s, real, imag)


def eigen_product(product, nev, split, width):
    for c in range(2):
        for half in range(2):
            at = (2 * c + half) * 2 * width
            done = product(slice(at, at + 2 * width))
            for q in range(2):
                split[c, pl.ds(2 * half + q, nev, stride=4), :] = done[:, q * width : (q + 1) * width]


def left_kernel(ident, sink, table, left, rows, *, depth):
    nev = table.shape[3]
    stack_rows(sink[0], sink[1], rows, depth)
    left[:, : rows.shape[0]] = rows[...].T
    for c in range(2):
        at = rows.shape[0] + c * 256
        left[:nev, at : at + nev] = table[ident[0], c]


def dress_kernel(gamma, tau, left, out, split, mixed):
    ndim, width = out.shape[1:]
    nev = ndim // 4
    for at in range(0, ndim, 2 * width):
        prop = dot(left[:, : 2 * ndim], tau[:, at : at + 2 * width]).astype(BF).astype(F32)
        split[0, at : at + 2 * width, :] = prop[:width].T
        split[1, at : at + 2 * width, :] = prop[width:].T

    def write(start, s, real, imag):
        rows = slice(start, start + TILE)
        low = slice(nev + start, nev + start + TILE)
        at_r = slice(s * width, (s + 1) * width)
        at_i = slice((4 + s) * width, (5 + s) * width)
        mixed[rows, at_r] = real.astype(BF)
        mixed[rows, at_i] = imag.astype(BF)
        mixed[low, at_r] = (-imag).astype(BF)
        mixed[low, at_i] = real.astype(BF)

    spin_mix(split, gamma, False, write, range(0, nev, TILE))
    real = left[:nev, 2 * ndim : 2 * ndim + nev]
    imag = left[:nev, 2 * ndim + 256 : 2 * ndim + 256 + nev]

    def product(at):
        return dot(real, mixed[:nev, at]) + dot(imag, mixed[nev:, at])

    eigen_product(product, nev, split, width)
    out[...] = split[...].astype(BF)


def prepare(d, block, gamma, tau, wide, mixed, rows, split, depth):
    ndim, width = block.shape[1:]
    nev = ndim // 4
    split[...] = block[...].astype(F32)

    def write(start, s, real, imag):
        top = slice(start, start + TILE)
        low = slice(nev + start, nev + start + TILE)
        at_r = slice(s * width, (s + 1) * width)
        at_i = slice((4 + s) * width, (5 + s) * width)
        mixed[d, top, at_r] = real.astype(BF)
        mixed[d, top, at_i] = imag.astype(BF)
        mixed[d, low, at_r] = imag.astype(BF)
        mixed[d, low, at_i] = (-real).astype(BF)

    spin_mix(split, gamma, True, write, range(0, nev, TILE))
    stack_rows(block[0], block[1], rows, depth)
    left = rows[...].T
    for at in range(0, ndim, 2 * width):
        product = dot(left, tau[:, at : at + 2 * width]).astype(BF)
        wide[d, :, at : at + 2 * width] = product[:width]
        wide[d, :, ndim + at : ndim + at + 2 * width] = product[width:]


def sort_kernel(tau, _, sorted_tau, order, chunk):
    ndim = tau.shape[1]
    nev = ndim // 4
    row = lax.broadcasted_iota(jnp.int32, (ndim, nev), 0)
    column = lax.broadcasted_iota(jnp.int32, (ndim, nev), 1)
    for s in range(4):
        order[:, s * nev : (s + 1) * nev] = (row == 4 * column + s).astype(F32).astype(BF)
    for turn, at in enumerate(range(0, 2 * ndim, 256)):
        chunk[turn % 2] = tau[at : at + 256, :]
        sorted_tau[at : at + 256, :] = dot(chunk[turn % 2], order[...]).astype(BF)


def own_kernel(gamma, tau, block, table, wide, mixed, fetched, rows, split, sem, *, depth):
    fetch = pltpu.make_async_copy(table, fetched, sem)
    fetch.start()
    prepare(0, block, gamma, tau, wide, mixed, rows, split, depth)
    fetch.wait()


def prepare_kernel(*refs, depth, entries):
    gamma, tau = refs[:2]
    blocks = refs[2 : 2 + len(entries)]
    wide, mixed, rows, split = refs[2 + len(entries) + 2 :]
    for turn, (d, block) in enumerate(zip(entries, blocks)):
        prepare(d, block, gamma, tau, wide, mixed, rows.at[turn], split.at[turn], depth)


def diagrams_kernel(
    meta, gamma, tau, last, backward, wide_in, mixed_in, out, wide, mixed,
    rows, split, column, totals, sem, *, depth,
):
    ndim, width = last.shape[1:]
    nev = ndim // 4
    slots = out.shape[0]
    count = meta[meta.shape[0] - 2]
    here = meta[meta.shape[0] - 1]
    scale = (2.0 * ndim) ** (-0.5)
    sign = 1 - 2 * (here % 2)

    def store(k):
        return pltpu.make_async_copy(totals.at[k], out.at[k], sem.at[k])

    @pl.when(count <= SURE)
    def _():
        totals[SURE:] = jnp.zeros((slots - SURE, *totals.shape[1:]), F32)
        for k in range(SURE, slots):
            store(k).start()

    def entry(sender):
        ahead = (sender - here) * sign
        near = jnp.where(ahead == 1, 1, 2)
        far = jnp.where(ahead == 2, 3, 4)
        return jnp.where(ahead == 0, 0, jnp.where(ahead * ahead == 1, near, far))

    def diagram(k):
        first = entry(meta[3 * k])
        second = entry(meta[3 * k + 1])
        table = backward.at[meta[3 * k + 2]]
        pair = column.at[k % 2]
        for half in range(2):
            at = 2 * half * width
            real = dot(table[...], mixed[first, :, at : at + 2 * width]).astype(BF)
            at += 4 * width
            imag = dot(table[...], mixed[first, :, at : at + 2 * width]).astype(BF)
            for q in range(2):
                s = 2 * half + q
                part = slice(q * width, (q + 1) * width)
                top = slice(s * nev, (s + 1) * nev)
                low = slice(ndim + s * nev, ndim + (s + 1) * nev)
                pair[top, :width] = real[:, part]
                pair[top, width:] = imag[:, part]
                pair[low, :width] = imag[:, part]
                pair[low, width:] = -real[:, part]
        result = dot(wide[second], pair[...]) * scale
        result = jnp.where(k < count, result, 0.0)
        totals[k, 0] = result[:, :width]
        totals[k, 1] = result[:, width:]
        store(k).start()

    prepare(3, last, gamma, tau, wide, mixed, rows, split, depth)
    for k in range(SURE):
        diagram(k)

    @pl.when(count > SURE)
    def _():
        for k in range(SURE, slots):
            diagram(k)

    for k in range(slots):
        store(k).wait()


def per_device(
    perambulator, elementals, sink_block, gamma_spin, graph_lists, diagram_counts, source_ids
):
    ndim, width = sink_block.shape[1:]
    slots = graph_lists.shape[1]
    nev = elementals.shape[3]
    depth = perambulator.shape[3]
    reach = 2 * DT + 1
    row_block = lax.all_to_all(perambulator, "col", split_axis=1, concat_axis=1, tiled=True)
    tau = row_block.reshape(2 * ndim, ndim)
    table = elementals[0]
    backward = jnp.concatenate(
        [jnp.swapaxes(table[:, 0], 1, 2), jnp.swapaxes(table[:, 1], 1, 2)], axis=2
    )
    smem = pl.BlockSpec(memory_space=pltpu.SMEM)
    vmem = pl.BlockSpec(memory_space=pltpu.VMEM)
    free = pl.BlockSpec(memory_space=pl.ANY)
    rows = pltpu.VMEM((2 * ndim, 2 * width), BF)
    split = pltpu.VMEM((2, ndim, width), F32)
    left = pl.pallas_call(
        functools.partial(left_kernel, depth=depth),
        out_shape=jax.ShapeDtypeStruct((2 * width, 2 * ndim + 512), BF),
        in_specs=[smem, vmem, vmem],
        out_specs=vmem,
        scratch_shapes=[rows],
        compiler_params=pltpu.CompilerParams(vmem_limit_bytes=8 << 20),
        name="left",
    )(source_ids, sink_block, table)
    gamma = jnp.broadcast_to(gamma_spin.reshape(-1, 1), (gamma_spin.size, width))
    position = lax.axis_index("src").astype(jnp.int32).reshape(1)
    meta = jnp.concatenate([graph_lists.reshape(-1), diagram_counts, position])
    tau, backward, left, gamma, meta = lax.optimization_barrier((tau, backward, left, gamma, meta))
    backward = pltpu.with_memory_space_constraint(backward, pltpu.HBM)

    dressed = pl.pallas_call(
        dress_kernel,
        out_shape=jax.ShapeDtypeStruct((2, ndim, width), BF),
        in_specs=[vmem, vmem, vmem],
        out_specs=vmem,
        scratch_shapes=[
            pltpu.VMEM((2, ndim, width), F32),
            pltpu.VMEM((2 * nev, 8 * width), BF),
        ],
        compiler_params=pltpu.CompilerParams(vmem_limit_bytes=10 << 20),
        name="dress",
    )(gamma, tau, left)
    state = (
        jax.ShapeDtypeStruct((reach, width, 2 * ndim), BF),
        jax.ShapeDtypeStruct((reach, 2 * nev, 8 * width), BF),
    )


    def prepared(blocks, entries, held):
        count = 2 + len(blocks)
        return pl.pallas_call(
            functools.partial(prepare_kernel, depth=depth, entries=entries),
            out_shape=state,
            in_specs=[vmem] * (2 + len(blocks) + len(held)),
            out_specs=(vmem, vmem),
            scratch_shapes=[
                pltpu.VMEM((len(blocks), *rows.shape), BF),
                pltpu.VMEM((len(blocks), *split.shape), F32),
            ],
            input_output_aliases={count: 0, count + 1: 1},
            compiler_params=pltpu.CompilerParams(vmem_limit_bytes=12 << 20),
            name="prepare",
        )(gamma, tau, *blocks, *held)

    even = swapped(dressed, "src", 0)
    odd = swapped(dressed, "src", 1)
    tau = pl.pallas_call(
        sort_kernel,
        out_shape=jax.ShapeDtypeStruct(tau.shape, BF),
        in_specs=[vmem, free],
        out_specs=vmem,
        scratch_shapes=[pltpu.VMEM((ndim, ndim), BF), pltpu.VMEM((2, 256, ndim), BF)],
        compiler_params=pltpu.CompilerParams(vmem_limit_bytes=8 << 20),
        input_output_aliases={0: 0},
        name="sort",
    )(tau, dressed)
    even, tau = lax.optimization_barrier((even, tau))
    odd_far = swapped(even, "src", 1)
    even_far = swapped(odd, "src", 0)
    *held, backward = pl.pallas_call(
        functools.partial(own_kernel, depth=depth),
        out_shape=(*state, jax.ShapeDtypeStruct(backward.shape, BF)),
        in_specs=[vmem, vmem, vmem, free],
        out_specs=(vmem, vmem, vmem),
        scratch_shapes=[rows, split, pltpu.SemaphoreType.DMA],
        compiler_params=pltpu.CompilerParams(vmem_limit_bytes=12 << 20),
        name="own",
    )(gamma, tau, dressed, backward)
    held = prepared((even, odd), (1, 2), held)
    held = prepared((odd_far,), (4,), held)
    totals, _, _ = pl.pallas_call(
        functools.partial(diagrams_kernel, depth=depth),
        out_shape=(jax.ShapeDtypeStruct((slots, 2, width, width), F32), *state),
        in_specs=[smem] + [vmem] * 6,
        out_specs=(free, vmem, vmem),
        scratch_shapes=[
            rows,
            split,
            pltpu.VMEM((2, 2 * ndim, 2 * width), BF),
            pltpu.VMEM((slots, 2, width, width), F32),
            pltpu.SemaphoreType.DMA((slots,)),
        ],
        input_output_aliases={5: 1, 6: 2},
        compiler_params=pltpu.CompilerParams(vmem_limit_bytes=16 << 20),
        name="diagrams",
    )(
        meta, gamma, tau, even_far, backward, *held
    )
    return totals[None, None]


def solution(mesh):
    in_specs = (
        P("src", None, None, "col", None),
        P("col", None, None, None, None),
        P(),
        P(),
        P("src", None, None),
        P("src"),
        P("src"),
    )
    out_specs = P("src", "col", None, None, None, None)
    return jax.shard_map(
        per_device, mesh=mesh, in_specs=in_specs, out_specs=out_specs, check_vma=False
    )
```

```python
import functools

import jax
import jax.numpy as jnp
from jax import lax
from jax.experimental import pallas as pl
from jax.experimental.pallas import tpu as pltpu
from jax.sharding import PartitionSpec as P

DT = 2
TILE = 16
SURE = 2
BF = jnp.bfloat16
F32 = jnp.float32


def swapped(shard, axis, start):
    count = lax.axis_size(axis)
    lower = range(start, count - 1, 2)
    return lax.ppermute(shard, axis, [(i, i + 1) for i in lower] + [(i + 1, i) for i in lower])


def dot(left, right):
    return jnp.dot(left, right, preferred_element_type=F32)


def stack_rows(real, imag, target, depth):
    width = real.shape[1]
    for at in range(0, real.shape[0], depth):
        upper = slice(2 * at, 2 * at + depth)
        lower = slice(2 * at + depth, 2 * at + 2 * depth)
        target[upper, :width] = real[at : at + depth]
        target[upper, width:] = imag[at : at + depth]
        target[lower, :width] = -imag[at : at + depth]
        target[lower, width:] = real[at : at + depth]


def spin_mix(split, gamma, adjoint, write, starts):
    for start in starts:
        part = [[split[c, pl.ds(4 * start + s, TILE, stride=4), :] for s in range(4)] for c in range(2)]
        for s in range(4):
            real = imag = None
            for q in range(4):
                at = 4 * q + s if adjoint else 4 * s + q
                g_r = gamma[pl.ds(at, TILE, stride=0), :]
                g_i = gamma[pl.ds(16 + at, TILE, stride=0), :]
                cross_r = g_i * part[1][q]
                cross_i = g_i * part[0][q]
                term_r = g_r * part[0][q] + cross_r if adjoint else g_r * part[0][q] - cross_r
                term_i = g_r * part[1][q] - cross_i if adjoint else g_r * part[1][q] + cross_i
                real = term_r if real is None else real + term_r
                imag = term_i if imag is None else imag + term_i
            write(start, s, real, imag)


def eigen_product(product, nev, split, width):
    for c in range(2):
        for half in range(2):
            at = (2 * c + half) * 2 * width
            done = product(slice(at, at + 2 * width))
            for q in range(2):
                split[c, pl.ds(2 * half + q, nev, stride=4), :] = done[:, q * width : (q + 1) * width]


def left_kernel(ident, sink, table, left, rows, *, depth):
    nev = table.shape[3]
    stack_rows(sink[0], sink[1], rows, depth)
    left[:, : rows.shape[0]] = rows[...].T
    left[:, rows.shape[0] :] = jnp.zeros((left.shape[0], left.shape[1] - rows.shape[0]), BF)
    for c in range(2):
        at = rows.shape[0] + c * 256
        left[:nev, at : at + nev] = table[ident[0], c]


def dress_kernel(gamma, tau, left, out, split, mixed):
    ndim, width = out.shape[1:]
    nev = ndim // 4
    for at in range(0, ndim, 2 * width):
        prop = dot(left[:, : 2 * ndim], tau[:, at : at + 2 * width]).astype(BF).astype(F32)
        split[0, at : at + 2 * width, :] = prop[:width].T
        split[1, at : at + 2 * width, :] = prop[width:].T

    def write(start, s, real, imag):
        rows = slice(start, start + TILE)
        low = slice(nev + start, nev + start + TILE)
        at_r = slice(s * width, (s + 1) * width)
        at_i = slice((4 + s) * width, (5 + s) * width)
        mixed[rows, at_r] = real.astype(BF)
        mixed[rows, at_i] = imag.astype(BF)
        mixed[low, at_r] = (-imag).astype(BF)
        mixed[low, at_i] = real.astype(BF)

    spin_mix(split, gamma, False, write, range(0, nev, TILE))
    real = left[:nev, 2 * ndim : 2 * ndim + nev]
    imag = left[:nev, 2 * ndim + 256 : 2 * ndim + 256 + nev]

    def product(at):
        return dot(real, mixed[:nev, at]) + dot(imag, mixed[nev:, at])

    eigen_product(product, nev, split, width)
    out[...] = split[...].astype(BF)


def prepare(d, block, gamma, tau, wide, mixed, rows, split, depth):
    ndim, width = block.shape[1:]
    nev = ndim // 4
    split[...] = block[...].astype(F32)

    def write(start, s, real, imag):
        top = slice(start, start + TILE)
        low = slice(nev + start, nev + start + TILE)
        at_r = slice(s * width, (s + 1) * width)
        at_i = slice((4 + s) * width, (5 + s) * width)
        mixed[d, top, at_r] = real.astype(BF)
        mixed[d, top, at_i] = imag.astype(BF)
        mixed[d, low, at_r] = imag.astype(BF)
        mixed[d, low, at_i] = (-real).astype(BF)

    stack_rows(block[0], block[1], rows, depth)
    left = rows[...].T
    share = nev // (ndim // (2 * width))
    for turn, at in enumerate(range(0, ndim, 2 * width)):
        spin_mix(split, gamma, True, write, range(turn * share, (turn + 1) * share, TILE))
        product = dot(left, tau[:, at : at + 2 * width]).astype(BF)
        wide[d, :, at : at + 2 * width] = product[:width]
        wide[d, :, ndim + at : ndim + at + 2 * width] = product[width:]


def sort_kernel(tau, _, sorted_tau, order, chunk):
    ndim = tau.shape[1]
    nev = ndim // 4
    row = lax.broadcasted_iota(jnp.int32, (ndim, nev), 0)
    column = lax.broadcasted_iota(jnp.int32, (ndim, nev), 1)
    for s in range(4):
        order[:, s * nev : (s + 1) * nev] = (row == 4 * column + s).astype(F32).astype(BF)
    for turn, at in enumerate(range(0, 2 * ndim, 256)):
        chunk[turn % 2] = tau[at : at + 256, :]
        sorted_tau[at : at + 256, :] = dot(chunk[turn % 2], order[...]).astype(BF)


def own_kernel(gamma, tau, block, table, wide, mixed, fetched, rows, split, sem, *, depth):
    fetch = pltpu.make_async_copy(table, fetched, sem)
    fetch.start()
    prepare(0, block, gamma, tau, wide, mixed, rows, split, depth)
    fetch.wait()


def prepare_kernel(*refs, depth, entries):
    gamma, tau = refs[:2]
    blocks = refs[2 : 2 + len(entries)]
    wide, mixed, rows, split = refs[2 + len(entries) + 2 :]
    for turn, (d, block) in enumerate(zip(entries, blocks)):
        prepare(d, block, gamma, tau, wide, mixed, rows.at[turn], split.at[turn], depth)


def diagrams_kernel(
    meta, gamma, tau, last, backward, wide_in, mixed_in, out, wide, mixed,
    rows, split, column, totals, sem, *, depth,
):
    ndim, width = last.shape[1:]
    nev = ndim // 4
    slots = out.shape[0]
    count = meta[meta.shape[0] - 2]
    here = meta[meta.shape[0] - 1]
    scale = (2.0 * ndim) ** (-0.5)
    sign = 1 - 2 * (here % 2)

    def store(k):
        return pltpu.make_async_copy(totals.at[k], out.at[k], sem.at[k])

    @pl.when(count <= SURE)
    def _():
        totals[SURE:] = jnp.zeros((slots - SURE, *totals.shape[1:]), F32)
        for k in range(SURE, slots):
            store(k).start()

    def entry(sender):
        ahead = (sender - here) * sign
        near = jnp.where(ahead == 1, 1, 2)
        far = jnp.where(ahead == 2, 3, 4)
        return jnp.where(ahead == 0, 0, jnp.where(ahead * ahead == 1, near, far))

    def diagram(k):
        first = entry(meta[3 * k])
        second = entry(meta[3 * k + 1])
        table = backward.at[meta[3 * k + 2]]
        pair = column.at[k % 2]
        for half in range(2):
            at = 2 * half * width
            real = dot(table[...], mixed[first, :, at : at + 2 * width]).astype(BF)
            at += 4 * width
            imag = dot(table[...], mixed[first, :, at : at + 2 * width]).astype(BF)
            for q in range(2):
                s = 2 * half + q
                part = slice(q * width, (q + 1) * width)
                top = slice(s * nev, (s + 1) * nev)
                low = slice(ndim + s * nev, ndim + (s + 1) * nev)
                pair[top, :width] = real[:, part]
                pair[top, width:] = imag[:, part]
                pair[low, :width] = imag[:, part]
                pair[low, width:] = -real[:, part]
        result = dot(wide[second], pair[...]) * scale
        result = jnp.where(k < count, result, 0.0)
        totals[k, 0] = result[:, :width]
        totals[k, 1] = result[:, width:]
        store(k).start()

    prepare(3, last, gamma, tau, wide, mixed, rows, split, depth)
    for k in range(SURE):
        diagram(k)

    @pl.when(count > SURE)
    def _():
        for k in range(SURE, slots):
            diagram(k)

    for k in range(slots):
        store(k).wait()


def per_device(
    perambulator, elementals, sink_block, gamma_spin, graph_lists, diagram_counts, source_ids
):
    ndim, width = sink_block.shape[1:]
    slots = graph_lists.shape[1]
    nev = elementals.shape[3]
    depth = perambulator.shape[3]
    reach = 2 * DT + 1
    row_block = lax.all_to_all(perambulator, "col", split_axis=1, concat_axis=1, tiled=True)
    tau = row_block.reshape(2 * ndim, ndim)
    table = elementals[0]
    backward = jnp.concatenate(
        [jnp.swapaxes(table[:, 0], 1, 2), jnp.swapaxes(table[:, 1], 1, 2)], axis=2
    )
    smem = pl.BlockSpec(memory_space=pltpu.SMEM)
    vmem = pl.BlockSpec(memory_space=pltpu.VMEM)
    free = pl.BlockSpec(memory_space=pl.ANY)
    rows = pltpu.VMEM((2 * ndim, 2 * width), BF)
    split = pltpu.VMEM((2, ndim, width), F32)
    left = pl.pallas_call(
        functools.partial(left_kernel, depth=depth),
        out_shape=jax.ShapeDtypeStruct((2 * width, 2 * ndim + 512), BF),
        in_specs=[smem, vmem, vmem],
        out_specs=vmem,
        scratch_shapes=[rows],
        compiler_params=pltpu.CompilerParams(vmem_limit_bytes=8 << 20),
        name="left",
    )(source_ids, sink_block, table)
    gamma = jnp.broadcast_to(gamma_spin.reshape(-1, 1), (gamma_spin.size, width))
    position = lax.axis_index("src").astype(jnp.int32).reshape(1)
    meta = jnp.concatenate([graph_lists.reshape(-1), diagram_counts, position])
    tau, backward, left, gamma, meta = lax.optimization_barrier((tau, backward, left, gamma, meta))
    backward = pltpu.with_memory_space_constraint(backward, pltpu.HBM)

    dressed = pl.pallas_call(
        dress_kernel,
        out_shape=jax.ShapeDtypeStruct((2, ndim, width), BF),
        in_specs=[vmem, vmem, vmem],
        out_specs=vmem,
        scratch_shapes=[
            pltpu.VMEM((2, ndim, width), F32),
            pltpu.VMEM((2 * nev, 8 * width), BF),
        ],
        compiler_params=pltpu.CompilerParams(vmem_limit_bytes=10 << 20),
        name="dress",
    )(gamma, tau, left)
    state = (
        jax.ShapeDtypeStruct((reach, width, 2 * ndim), BF),
        jax.ShapeDtypeStruct((reach, 2 * nev, 8 * width), BF),
    )


    def prepared(blocks, entries, held):
        count = 2 + len(blocks)
        return pl.pallas_call(
            functools.partial(prepare_kernel, depth=depth, entries=entries),
            out_shape=state,
            in_specs=[vmem] * (2 + len(blocks) + len(held)),
            out_specs=(vmem, vmem),
            scratch_shapes=[
                pltpu.VMEM((len(blocks), *rows.shape), BF),
                pltpu.VMEM((len(blocks), *split.shape), F32),
            ],
            input_output_aliases={count: 0, count + 1: 1},
            compiler_params=pltpu.CompilerParams(vmem_limit_bytes=12 << 20),
            name="prepare",
        )(gamma, tau, *blocks, *held)

    even = swapped(dressed, "src", 0)
    odd = swapped(dressed, "src", 1)
    tau = pl.pallas_call(
        sort_kernel,
        out_shape=jax.ShapeDtypeStruct(tau.shape, BF),
        in_specs=[vmem, free],
        out_specs=vmem,
        scratch_shapes=[pltpu.VMEM((ndim, ndim), BF), pltpu.VMEM((2, 256, ndim), BF)],
        compiler_params=pltpu.CompilerParams(vmem_limit_bytes=8 << 20),
        input_output_aliases={0: 0},
        name="sort",
    )(tau, dressed)
    even, tau = lax.optimization_barrier((even, tau))
    odd_far = swapped(even, "src", 1)
    even_far = swapped(odd, "src", 0)
    *held, backward = pl.pallas_call(
        functools.partial(own_kernel, depth=depth),
        out_shape=(*state, jax.ShapeDtypeStruct(backward.shape, BF)),
        in_specs=[vmem, vmem, vmem, free],
        out_specs=(vmem, vmem, vmem),
        scratch_shapes=[rows, split, pltpu.SemaphoreType.DMA],
        compiler_params=pltpu.CompilerParams(vmem_limit_bytes=12 << 20),
        name="own",
    )(gamma, tau, dressed, backward)
    held = prepared((even, odd), (1, 2), held)
    held = prepared((odd_far,), (4,), held)
    totals, _, _ = pl.pallas_call(
        functools.partial(diagrams_kernel, depth=depth),
        out_shape=(jax.ShapeDtypeStruct((slots, 2, width, width), F32), *state),
        in_specs=[smem] + [vmem] * 6,
        out_specs=(free, vmem, vmem),
        scratch_shapes=[
            rows,
            split,
            pltpu.VMEM((2, 2 * ndim, 2 * width), BF),
            pltpu.VMEM((slots, 2, width, width), F32),
            pltpu.SemaphoreType.DMA((slots,)),
        ],
        input_output_aliases={5: 1, 6: 2},
        compiler_params=pltpu.CompilerParams(vmem_limit_bytes=16 << 20),
        name="diagrams",
    )(
        meta, gamma, tau, even_far, backward, *held
    )
    return totals[None, None]


def solution(mesh):
    in_specs = (
        P("src", None, None, "col", None),
        P("col", None, None, None, None),
        P(),
        P(),
        P("src", None, None),
        P("src"),
        P("src"),
    )
    out_specs = P("src", "col", None, None, None, None)
    return jax.shard_map(
        per_device, mesh=mesh, in_specs=in_specs, out_specs=out_specs, check_vma=False
    )
```
